32 devices in a mesh: groups: 2 (over x), img: 16 (over z, y, core).
Axes of the slice: x: 2, y: 2, z: 4, core: 2. Of those that a mesh axis runs over, the one named last changes fastest.
Arguments:
- images: bfloat16 [256, 4608], P(('groups', 'img')), parts along dimension 0, may hold values from -64 to 64
- class_refs: bfloat16 [96, 4608], P('groups', 'img'), parts along dimension 0, may hold values from -0.6 to 0.6
- sigma2: float32 [32, 16], P('groups'), parts along dimension 0, may hold values from 0.5 to 18
- ctf_group: int32 [256], P(('groups', 'img')), parts along dimension 0, may hold values from 0 to 15, as said below
- defocus_bin: int32 [256], P(('groups', 'img')), parts along dimension 0, may hold values from 0 to 31
Outputs:
- new_refs: float32 [96, 4608], P('groups', 'img'), parts along dimension 0
The draws below stay inside these ranges and needn't reach their ends.
There are 2 independent parts, one for each index of `groups`. The reference program is written for one: setup_inputs(seed, part) draws one part's arguments, and reference() takes and returns one part's arrays. A program takes and returns all parts, laid end to end along the dimension named above; each array names one. Nothing has to cross between parts.
Inputs may be any that keep to these rules, and one draw needn't show every extreme that they name: `ctf_group`: never falls from one image to the next; every group appears.
All inputs are finite; a program needn't handle non-finite values.
Results may differ from the reference program's by a relative error of at most 0.0084.
Values may be sent and summed in bfloat16 or wider, within the bound.
A program may use at most 128 MiB of HBM per device.

```python
import math
import jax
import jax.numpy as jnp
from jax import lax

CLASSES = 48
ROT = 36
SHELLS = 16
ANG = 144
REACH = 3
SHIFTS = 49
BINS = 32
NGROUP = 16
IMAGES = 128


def group_ids(key):
    extra = jax.random.randint(jax.random.fold_in(key, 11), (IMAGES - NGROUP,), 0, NGROUP)
    joined = jnp.concatenate([jnp.arange(NGROUP, dtype=jnp.int32), extra.astype(jnp.int32)])
    return jnp.sort(joined)


def bin_ids(key):
    return jax.random.randint(jax.random.fold_in(key, 13), (IMAGES,), 0, BINS).astype(jnp.int32)


def noise_table(key, rise):
    level = jnp.arange(NGROUP, dtype=jnp.float32) / max(NGROUP - 1, 1)
    base = jnp.exp(jax.random.uniform(jax.random.fold_in(key, 17), (NGROUP, SHELLS), jnp.float32, math.log(0.5), math.log(2.0)))
    return base * rise ** level[:, None]


def reference_table(key):
    values = jax.random.normal(jax.random.fold_in(key, 21), (CLASSES, 2, SHELLS, ANG), jnp.float32)
    return 0.1 * jnp.clip(values, -6.0, 6.0)


def draw_ctf_group(key, part):
    return group_ids(key)


def draw_defocus_bin(key, part):
    return bin_ids(key)


def draw_sigma2(key, part):
    return noise_table(key, 3.0)


def draw_class_refs(key, part):
    table = reference_table(key)
    return table.reshape(CLASSES, 2 * SHELLS * ANG).astype(jnp.bfloat16)


def draw_images(key, part):
    values = jax.random.normal(jax.random.fold_in(key, 31), (IMAGES, 2 * SHELLS * ANG), jnp.float32)
    return jnp.clip(values, -6.0, 6.0).astype(jnp.bfloat16)


def setup_inputs(seed: int = 0, part: int = 0) -> dict:
    keys = jax.random.split(jax.random.key(seed), 6)
    part_keys = jax.random.split(jax.random.fold_in(keys[5], part), 6)
    images = draw_images(jax.random.fold_in(jax.random.fold_in(keys[5], part), 71), part)
    class_refs = draw_class_refs(jax.random.fold_in(jax.random.fold_in(keys[5], part), 71), part)
    sigma2 = draw_sigma2(jax.random.fold_in(jax.random.fold_in(keys[5], part), 71), part)
    ctf_group = draw_ctf_group(jax.random.fold_in(jax.random.fold_in(keys[5], part), 71), part)
    defocus_bin = draw_defocus_bin(jax.random.fold_in(jax.random.fold_in(keys[5], part), 71), part)
    return dict(images=images, class_refs=class_refs, sigma2=sigma2, ctf_group=ctf_group, defocus_bin=defocus_bin)


def shell_radius():
    return (jnp.arange(SHELLS, dtype=jnp.float32) + 1.0) / (2.0 * SHELLS)


def ctf_table():
    defocus = 1.0 + jnp.arange(BINS, dtype=jnp.float32) / BINS
    radius = shell_radius()
    return -jnp.sin(80.0 * defocus[:, None] * radius[None, :] ** 2 + 0.1)


def phase_tables():
    offsets = jnp.arange(2 * REACH + 1, dtype=jnp.float32) - REACH
    shift_x = jnp.repeat(offsets, 2 * REACH + 1)
    shift_y = jnp.tile(offsets, 2 * REACH + 1)
    angles = 2.0 * math.pi * jnp.arange(ANG, dtype=jnp.float32) / ANG
    radius = shell_radius()
    phase = 2.0 * math.pi * radius[None, :, None] * (
        jnp.cos(angles)[None, None, :] * shift_x[:, None, None]
        + jnp.sin(angles)[None, None, :] * shift_y[:, None, None])
    return jnp.cos(phase), jnp.sin(phase)


def image_weights(ctf_group, defocus_bin, sigma2):
    bin_hot = (defocus_bin[:, None] == jnp.arange(BINS, dtype=jnp.int32)[None, :]).astype(jnp.float32)
    group_hot = (ctf_group[:, None] == jnp.arange(NGROUP, dtype=jnp.int32)[None, :]).astype(jnp.float32)
    ctf_sel = jnp.dot(bin_hot, ctf_table(), precision=lax.Precision.HIGHEST)
    noise_sel = jnp.dot(group_hot, sigma2, precision=lax.Precision.HIGHEST)
    return ctf_sel / noise_sel, ctf_sel * ctf_sel / noise_sel


def shifted_features(images, filter_weight):
    count_img = images.shape[0]
    pixels = images.astype(jnp.float32).reshape(count_img, 2, SHELLS, ANG)
    real_part = pixels[:, 0] * filter_weight[:, :, None]
    imag_part = pixels[:, 1] * filter_weight[:, :, None]
    cosine, sine_table = phase_tables()
    shifted_real = real_part[:, None] * cosine[None] - imag_part[:, None] * sine_table[None]
    shifted_imag = real_part[:, None] * sine_table[None] + imag_part[:, None] * cosine[None]
    stacked = jnp.stack([shifted_real, shifted_imag], axis=2)
    return stacked.reshape(count_img * SHIFTS, 2 * SHELLS * ANG).astype(jnp.bfloat16)


def reference(images, class_refs, sigma2, ctf_group, defocus_bin):
    count_img = images.shape[0]
    angle_step = ANG // ROT
    filter_weight, shell_weight = image_weights(ctf_group, defocus_bin, sigma2)
    features = shifted_features(images, filter_weight)
    refs_four = class_refs.reshape(CLASSES, 2, SHELLS, ANG)
    rotated = jnp.concatenate([jnp.roll(refs_four, turn_index * angle_step, axis=3) for turn_index in range(ROT)], axis=0)
    rotated = rotated.reshape(ROT * CLASSES, 2 * SHELLS * ANG)
    cross = jnp.dot(features, rotated.T, preferred_element_type=jnp.float32)
    shell_power = jnp.sum(jnp.square(refs_four.astype(jnp.float32)), axis=(1, 3))
    quadratic = 0.5 * jnp.dot(shell_weight, shell_power.T, precision=lax.Precision.HIGHEST)
    scores = cross.reshape(count_img, SHIFTS, ROT, CLASSES) - quadratic[:, None, None, :]
    highest = jnp.max(scores, axis=(1, 2, 3), keepdims=True)
    expanded = jnp.exp(scores - highest)
    normalizer = jnp.sum(expanded, axis=(1, 2, 3), keepdims=True)
    posterior = expanded / normalizer
    occupancy = jnp.sum(posterior, axis=(1, 2))
    posterior_b = posterior.astype(jnp.bfloat16).reshape(count_img * SHIFTS, ROT * CLASSES)
    oriented = jnp.dot(posterior_b.T, features, preferred_element_type=jnp.float32)
    oriented = oriented.reshape(ROT, CLASSES, 2, SHELLS, ANG)
    numerator = jnp.zeros((CLASSES, 2, SHELLS, ANG), jnp.float32)
    for turn_index in range(ROT):
        numerator = numerator + jnp.roll(oriented[turn_index], -turn_index * angle_step, axis=3)
    weights = jnp.dot(occupancy.T, shell_weight, precision=lax.Precision.HIGHEST)
    new_refs = numerator / (weights[:, None, :, None] + 1.0)
    return new_refs.reshape(CLASSES, 2 * SHELLS * ANG)
```

```python
import math

import jax
import jax.numpy as jnp
from jax import lax
from jax.experimental import pallas as pl
from jax.experimental.pallas import tpu as pltpu
from jax.sharding import PartitionSpec as P

CLASSES = 48
ROT = 36
SHELLS = 16
ANG = 144
REACH = 3
SHIFTS = 49
BINS = 32
NGROUP = 16


def shell_radius():
    return (jnp.arange(SHELLS, dtype=jnp.float32) + 1.0) / (2.0 * SHELLS)


def ctf_table():
    defocus = 1.0 + jnp.arange(BINS, dtype=jnp.float32) / BINS
    radius = shell_radius()
    return -jnp.sin(80.0 * defocus[:, None] * radius[None, :] ** 2 + 0.1)


def angle_major(values):
    count = values.shape[0]
    return (
        values.reshape(count, 2, SHELLS, ANG).transpose(0, 3, 1, 2).reshape(count, 2 * SHELLS * ANG)
    )


def shell_major(values):
    count = values.shape[0]
    return (
        values.reshape(count, ANG, 2, SHELLS).transpose(0, 2, 3, 1).reshape(count, 2 * SHELLS * ANG)
    )


def phase_flat():
    offsets = jnp.arange(2 * REACH + 1, dtype=jnp.float32) - REACH
    shift_x = jnp.repeat(offsets, 2 * REACH + 1)
    shift_y = jnp.tile(offsets, 2 * REACH + 1)
    angles = 2.0 * math.pi * jnp.arange(ANG, dtype=jnp.float32) / ANG
    radius = shell_radius()
    phase = (
        2.0
        * math.pi
        * radius[None, None, :]
        * (
            jnp.cos(angles)[None, :, None] * shift_x[:, None, None]
            + jnp.sin(angles)[None, :, None] * shift_y[:, None, None]
        )
    )
    cosine = jnp.cos(phase)
    sine_table = jnp.sin(phase)
    cos_flat = jnp.stack([cosine, cosine], axis=2).reshape(SHIFTS, 2 * SHELLS * ANG)
    sin_flat = jnp.stack([-sine_table, sine_table], axis=2).reshape(SHIFTS, 2 * SHELLS * ANG)
    return (cos_flat, sin_flat)


def image_weights(ctf_group, defocus_bin, sigma2):
    bin_hot = (defocus_bin[:, None] == jnp.arange(BINS, dtype=jnp.int32)[None, :]).astype(
        jnp.float32
    )
    group_hot = (ctf_group[:, None] == jnp.arange(NGROUP, dtype=jnp.int32)[None, :]).astype(
        jnp.float32
    )
    ctf_sel = jnp.dot(bin_hot, ctf_table(), precision=lax.Precision.HIGHEST)
    noise_sel = jnp.dot(group_hot, sigma2, precision=lax.Precision.HIGHEST)
    return (ctf_sel / noise_sel, ctf_sel * ctf_sel / noise_sel)


LANES = 128
STEP = ANG // ROT
SPAN = STEP * 2 * SHELLS
WIDTH = ROT * SPAN
BIG = 1e30


def fold_lanes(row, count_img, combine):
    cols = row.shape[1]
    total = row[:, :LANES]
    for start in range(LANES, cols, LANES):
        total = combine(total, row[:, start : start + LANES])
    reach = count_img
    while reach < LANES:
        total = combine(total, pltpu.roll(total, reach, 1))
        reach *= 2
    return jnp.concatenate([total] * (cols // LANES), axis=1)


def em_kernel(
    count_img,
    refs_ref,
    img_ref,
    fw_ref,
    cos_ref,
    sin_ref,
    sw_ref,
    num_ref,
    field_ref,
    feats,
    twice,
    scores,
    post,
    acc,
):
    rows = CLASSES
    cols = feats.shape[0]
    used = SHIFTS * count_img
    filtered = img_ref[...].astype(jnp.float32) * jnp.concatenate([fw_ref[...]] * ROT, axis=1)
    lane = lax.broadcasted_iota(jnp.int32, (count_img, WIDTH), 1)
    real_lane = lax.rem(lane, 2 * SHELLS) < SHELLS
    swapped = jnp.where(
        real_lane,
        pltpu.roll(filtered, WIDTH - SHELLS, 1),
        pltpu.roll(filtered, SHELLS, 1),
    )

    def shifted(shift):
        cosine = cos_ref[pl.ds(shift, 1), :]
        sine = sin_ref[pl.ds(shift, 1), :]
        return filtered * cosine + swapped * sine

    def feature_pair(pair, carry):
        first = shifted(2 * pair)
        second = shifted(2 * pair + 1)
        start = pl.multiple_of(pair * 2 * count_img, 2 * count_img)
        feats[pl.ds(start, 2 * count_img), :] = jnp.concatenate([first, second], axis=0).astype(
            jnp.bfloat16
        )
        return carry

    lax.fori_loop(0, SHIFTS // 2, feature_pair, 0)
    last = shifted(SHIFTS - 1)
    feats[used - count_img : used + count_img, :] = jnp.concatenate(
        [last, jnp.zeros_like(last)], axis=0
    ).astype(jnp.bfloat16)
    feats[used + count_img :, :] = jnp.zeros((cols - used - count_img, WIDTH), jnp.bfloat16)

    refs = refs_ref[...]
    twice[:, :WIDTH] = refs
    twice[:, WIDTH:] = refs
    power = jnp.zeros((rows, SPAN), jnp.float32)
    for block in range(ROT):
        piece = refs_ref[:, block * SPAN : (block + 1) * SPAN].astype(jnp.float32)
        power = power + piece * piece
    quad = 0.5 * lax.dot_general(
        power,
        sw_ref[...],
        (((1,), (0,)), ((), ())),
        precision=lax.Precision.HIGHEST,
        preferred_element_type=jnp.float32,
    )
    col = lax.broadcasted_iota(jnp.int32, (rows, cols), 1)
    quad = jnp.where(col < used, quad, BIG)

    depth = 4 * SPAN
    for turn in range(ROT):
        scores[turn * rows : (turn + 1) * rows, :] = -quad

    def cross_step(step, carry):
        base = pl.multiple_of(step * depth, depth)
        left = jnp.concatenate(
            [
                twice[:, pl.ds(pl.multiple_of(base + (ROT - turn) * SPAN, SPAN), depth)]
                for turn in range(ROT)
            ],
            axis=0,
        )
        scores[...] += lax.dot_general(
            left,
            feats[:, pl.ds(base, depth)],
            (((1,), (1,)), ((), ())),
            preferred_element_type=jnp.float32,
        )
        return carry

    lax.fori_loop(0, WIDTH // depth, cross_step, 0)

    def max_step(turn, best):
        start = pl.multiple_of(turn * rows, rows)
        return jnp.maximum(best, scores[pl.ds(start, rows), :])

    best = lax.fori_loop(0, ROT, max_step, jnp.full((rows, cols), -BIG, jnp.float32))
    top = fold_lanes(jnp.max(best, axis=0, keepdims=True), count_img, jnp.maximum)

    def exp_step(turn, total):
        start = pl.multiple_of(turn * rows, rows)
        value = jnp.exp(scores[pl.ds(start, rows), :] - top)
        scores[pl.ds(start, rows), :] = value
        return total + value

    total = lax.fori_loop(0, ROT, exp_step, jnp.zeros((rows, cols), jnp.float32))
    norm = fold_lanes(jnp.sum(total, axis=0, keepdims=True), count_img, jnp.add)
    scale = 1.0 / norm

    def post_step(turn, carry):
        start = pl.multiple_of(turn * rows, rows)
        post[pl.ds(start, rows), :] = (scores[pl.ds(start, rows), :] * scale).astype(jnp.bfloat16)
        return carry

    lax.fori_loop(0, ROT, post_step, 0)
    field_ref[...] = lax.dot_general(
        total * scale,
        sw_ref[...],
        (((1,), (1,)), ((), ())),
        precision=lax.Precision.HIGHEST,
        preferred_element_type=jnp.float32,
    )

    acc[...] = jnp.zeros_like(acc)
    wide = 2 * SPAN

    def back_step(step, carry):
        base = pl.multiple_of(step * wide, wide)
        oriented = jnp.dot(
            post[...], feats[:, pl.ds(base, wide)], preferred_element_type=jnp.float32
        )
        for turn in range(ROT):
            where = pl.ds(pl.multiple_of(base + (ROT - turn) * SPAN, SPAN), wide)
            acc[:, where] += oriented[turn * rows : (turn + 1) * rows]
        return carry

    lax.fori_loop(0, WIDTH // wide, back_step, 0)
    num_ref[...] = acc[:, :WIDTH] + acc[:, WIDTH:]


def em_step(refs_angle, images_angle, filter_weight, shell_weight):
    count_img = images_angle.shape[0]
    cols = -(-(SHIFTS + 1) * count_img // LANES) * LANES
    repeats = SPAN // SHELLS
    cos_flat, sin_flat = phase_flat()
    weight_rows = jnp.pad(jnp.tile(shell_weight.T, (repeats, SHIFTS)), ((0, 0), (0, cols - SHIFTS * count_img)))
    return pl.pallas_call(
        lambda *refs: em_kernel(count_img, *refs),
        out_shape=(
            jax.ShapeDtypeStruct((CLASSES, WIDTH), jnp.float32),
            jax.ShapeDtypeStruct((CLASSES, SPAN), jnp.float32),
        ),
        in_specs=[pl.BlockSpec(memory_space=pltpu.VMEM)] * 6,
        out_specs=(pl.BlockSpec(memory_space=pltpu.VMEM),) * 2,
        scratch_shapes=[
            pltpu.VMEM((cols, WIDTH), jnp.bfloat16),
            pltpu.VMEM((CLASSES, 2 * WIDTH), jnp.bfloat16),
            pltpu.VMEM((ROT * CLASSES, cols), jnp.float32),
            pltpu.VMEM((ROT * CLASSES, cols), jnp.bfloat16),
            pltpu.VMEM((CLASSES, 2 * WIDTH), jnp.float32),
        ],
        compiler_params=pltpu.CompilerParams(vmem_limit_bytes=60 * 2**20),
        name="em_step",
    )(
        refs_angle,
        images_angle,
        jnp.tile(filter_weight, (1, repeats)),
        cos_flat,
        sin_flat,
        weight_rows,
    )


def on_device(images, class_refs, sigma2, ctf_group, defocus_bin):
    width = 2 * SHELLS * ANG
    whole_refs = lax.all_gather(class_refs, "img", axis=1, tiled=True)
    refs_angle = angle_major(whole_refs)
    filter_weight, shell_weight = image_weights(ctf_group, defocus_bin, sigma2)
    numerator, field = em_step(refs_angle, angle_major(images), filter_weight, shell_weight)
    numerator = shell_major(numerator)
    local_weights = field[:, :SHELLS]
    share_cols = width // lax.axis_size("img")
    offset = lax.axis_index("img") * share_cols
    numerator_share = lax.psum_scatter(numerator, "img", scatter_dimension=1, tiled=True)
    weights = lax.psum(local_weights, "img")
    weight_field = jnp.broadcast_to(weights[:, None, :, None], (CLASSES, 2, SHELLS, ANG)).reshape(
        CLASSES, width
    )
    field_share = lax.dynamic_slice_in_dim(weight_field, offset, share_cols, 1)
    return numerator_share / (field_share + 1.0)


def solution(mesh):
    in_specs = (
        P(("groups", "img"), None),
        P("groups", "img"),
        P("groups", None),
        P(("groups", "img")),
        P(("groups", "img")),
    )
    out_specs = P("groups", "img")
    return jax.shard_map(
        on_device, mesh=mesh, in_specs=in_specs, out_specs=out_specs, check_vma=False
    )
```

```python
import math

import jax
import jax.numpy as jnp
import numpy as np
from jax import lax
from jax.experimental import pallas as pl
from jax.experimental.pallas import tpu as pltpu
from jax.sharding import PartitionSpec as P

CLASSES = 48
ROT = 36
SHELLS = 16
ANG = 144
REACH = 3
SHIFTS = 49
BINS = 32
NGROUP = 16


def shell_radius():
    return (jnp.arange(SHELLS, dtype=jnp.float32) + 1.0) / (2.0 * SHELLS)


def ctf_table():
    defocus = 1.0 + jnp.arange(BINS, dtype=jnp.float32) / BINS
    radius = shell_radius()
    return -jnp.sin(80.0 * defocus[:, None] * radius[None, :] ** 2 + 0.1)


def image_weights(ctf_group, defocus_bin, sigma2):
    bin_hot = (defocus_bin[:, None] == jnp.arange(BINS, dtype=jnp.int32)[None, :]).astype(
        jnp.float32
    )
    group_hot = (ctf_group[:, None] == jnp.arange(NGROUP, dtype=jnp.int32)[None, :]).astype(
        jnp.float32
    )
    ctf_sel = jnp.dot(bin_hot, ctf_table(), precision=lax.Precision.HIGHEST)
    noise_sel = jnp.dot(group_hot, sigma2, precision=lax.Precision.HIGHEST)
    return (ctf_sel / noise_sel, ctf_sel * ctf_sel / noise_sel)


LANES = 128
PARTS = 2 * SHELLS
SPAN = ANG // ROT * PARTS
WIDTH = ROT * SPAN
SIDE = 2 * REACH + 1
SLOTS = SIDE + 1
BIG = 1e30


def phase_parts():
    offsets = np.arange(SIDE) - REACH
    angles = 2.0 * np.pi * np.arange(ANG) / ANG
    radius = (np.arange(SHELLS) + 1.0) / (2.0 * SHELLS)
    tables = []
    for direction in (np.cos(angles), np.sin(angles)):
        phase = 2.0 * np.pi * offsets[:, None, None] * direction[None, :, None] * radius
        cosine, sine = np.cos(phase), np.sin(phase)
        tables.append(np.stack([cosine, cosine], axis=2).reshape(SIDE, WIDTH))
        tables.append(np.stack([-sine, sine], axis=2).reshape(SIDE, WIDTH))
    return np.stack(tables).astype(np.float32)


def fold_lanes(row, count_img, combine):
    cols = row.shape[1]
    total = row[:, :LANES]
    for start in range(LANES, cols, LANES):
        total = combine(total, row[:, start : start + LANES])
    reach = count_img
    while reach < LANES:
        total = combine(total, pltpu.roll(total, reach, 1))
        reach *= 2
    return jnp.concatenate([total] * (cols // LANES), axis=1)


def em_kernel(
    count_dev,
    img_ref,
    refs_ref,
    fw_ref,
    phase_ref,
    sw_ref,
    out_ref,
    feats,
    twice,
    scores,
    post,
    acc,
    turned_img,
    turned,
    turned_field,
    partial,
    got,
    pay,
    mid,
    mixed,
    final,
    near_send,
    near_recv,
    far_send,
    far_recv,
    pair_send,
    pair_recv,
    last_send,
    last_recv,
):
    rows = CLASSES
    count_img = img_ref.shape[0]
    share = refs_ref.shape[1]
    cols = feats.shape[0]
    half = count_dev // 2
    piece = min(share, ANG)
    pieces = share // piece
    me = lax.axis_index("img")
    core = lax.rem(me, 2)
    place = lax.div(me, 2)
    partner = me + 1 - 2 * core

    def ahead(offset):
        return lax.rem(place + offset, half)

    def behind(offset):
        return lax.rem(place + half - offset, half)

    barrier = pltpu.get_barrier_semaphore()
    for offset in range(1, half):
        pl.semaphore_signal(
            barrier,
            inc=1,
            device_id={"img": 2 * ahead(offset) + core},
            device_id_type=pl.DeviceIdType.MESH,
        )
    pl.semaphore_signal(
        barrier, inc=1, device_id={"img": partner}, device_id_type=pl.DeviceIdType.MESH
    )
    pl.semaphore_wait(barrier, half)

    def remote(source, target, send, recv, device):
        return pltpu.make_async_remote_copy(
            src_ref=source,
            dst_ref=target,
            send_sem=send,
            recv_sem=recv,
            device_id={"img": device},
            device_id_type=pl.DeviceIdType.MESH,
        )

    far = [
        remote(
            refs_ref,
            got.at[me],
            far_send.at[offset],
            far_recv.at[offset],
            2 * ahead(offset) + core,
        )
        for offset in range(1, half)
    ]
    near = [remote(refs_ref, got.at[me], near_send.at[0], near_recv.at[0], partner)]
    for copy in far + near:
        copy.start()

    for part in range(PARTS):
        block = img_ref[:, part * ANG : (part + 1) * ANG].astype(jnp.float32)
        turned_img[pl.ds(part, ANG, stride=PARTS), :] = block.T
    weight = fw_ref[...]
    lane = lax.broadcasted_iota(jnp.int32, (count_img, WIDTH), 1)
    real_lane = lax.rem(lane, PARTS) < SHELLS

    def swap(value):
        return jnp.where(
            real_lane, pltpu.roll(value, WIDTH - SHELLS, 1), pltpu.roll(value, SHELLS, 1)
        )

    filtered = jnp.concatenate(
        [turned_img[q * SPAN : (q + 1) * SPAN, :].T * weight for q in range(ROT)], axis=1
    )
    partial[0] = filtered
    partial[1] = swap(filtered)
    group = SLOTS * count_img

    def feature_step(step, carry):
        moved = (
            partial[0] * phase_ref[0, pl.ds(step, 1), :]
            + partial[1] * phase_ref[1, pl.ds(step, 1), :]
        )
        partial[2] = moved
        partial[3] = swap(moved)
        start = pl.multiple_of(step * group, group)
        for slot in range(0, SLOTS, 2):
            pair = []
            for shift in (slot, slot + 1):
                if shift < SIDE:
                    pair.append(
                        partial[2] * phase_ref[2, shift : shift + 1, :]
                        + partial[3] * phase_ref[3, shift : shift + 1, :]
                    )
                else:
                    pair.append(jnp.zeros((count_img, WIDTH), jnp.float32))
            feats[pl.ds(start + slot * count_img, 2 * count_img), :] = jnp.concatenate(
                pair, axis=0
            ).astype(jnp.bfloat16)
        return carry

    lax.fori_loop(0, SIDE, feature_step, 0)
    feats[SIDE * group :, :] = jnp.zeros((cols - SIDE * group, WIDTH), jnp.bfloat16)

    def place_refs(block, source):
        block = block.astype(jnp.float32)
        for index in range(pieces):
            first = source * share + index * piece
            start = lax.rem(first, ANG) * PARTS + lax.div(first, ANG)
            turned[pl.ds(start, piece, stride=PARTS), :] = block[
                :, index * piece : (index + 1) * piece
            ].T

    for offset in range(1, half):
        source = 2 * behind(offset) + core
        far[offset - 1].wait_recv()
        copy = remote(
            got.at[source], got.at[source], near_send.at[offset], near_recv.at[offset], partner
        )
        copy.start()
        near.append(copy)
    place_refs(refs_ref[...], me)
    for offset in range(1, half):
        source = 2 * behind(offset) + core
        place_refs(got[source], source)
    for offset in range(half):
        source = 2 * behind(offset) + 1 - core
        near[offset].wait_recv()
        place_refs(got[source], source)
    for copy in far + near:
        copy.wait_send()

    power = jnp.zeros((rows, SPAN), jnp.float32)
    for q in range(ROT):
        block = turned[q * SPAN : (q + 1) * SPAN, :].T
        power = power + block * block
        block = block.astype(jnp.bfloat16)
        twice[:, q * SPAN : (q + 1) * SPAN] = block
        twice[:, WIDTH + q * SPAN : WIDTH + (q + 1) * SPAN] = block
    quad = 0.5 * lax.dot_general(
        power,
        sw_ref[...],
        (((1,), (0,)), ((), ())),
        precision=lax.Precision.HIGHEST,
        preferred_element_type=jnp.float32,
    )
    col = lax.broadcasted_iota(jnp.int32, (rows, cols), 1)
    used = (lax.rem(col, group) < SIDE * count_img) & (col < SIDE * group)
    quad = jnp.where(used, quad, BIG)

    depth = 4 * SPAN
    for turn in range(ROT):
        scores[turn * rows : (turn + 1) * rows, :] = -quad

    def cross_step(step, carry):
        base = pl.multiple_of(step * depth, depth)
        left = jnp.concatenate(
            [
                twice[:, pl.ds(pl.multiple_of(base + (ROT - turn) * SPAN, SPAN), depth)]
                for turn in range(ROT)
            ],
            axis=0,
        )
        scores[...] += lax.dot_general(
            left,
            feats[:, pl.ds(base, depth)],
            (((1,), (1,)), ((), ())),
            preferred_element_type=jnp.float32,
        )
        return carry

    lax.fori_loop(0, WIDTH // depth, cross_step, 0)

    def max_step(turn, best):
        start = pl.multiple_of(turn * rows, rows)
        return jnp.maximum(best, scores[pl.ds(start, rows), :])

    best = lax.fori_loop(0, ROT, max_step, jnp.full((rows, cols), -BIG, jnp.float32))
    top = fold_lanes(jnp.max(best, axis=0, keepdims=True), count_img, jnp.maximum)

    def exp_step(turn, total):
        start = pl.multiple_of(turn * rows, rows)
        value = jnp.exp(scores[pl.ds(start, rows), :] - top)
        scores[pl.ds(start, rows), :] = value
        return total + value

    total = lax.fori_loop(0, ROT, exp_step, jnp.zeros((rows, cols), jnp.float32))
    norm = fold_lanes(jnp.sum(total, axis=0, keepdims=True), count_img, jnp.add)
    scale = 1.0 / norm

    def post_step(turn, carry):
        start = pl.multiple_of(turn * rows, rows)
        post[pl.ds(start, rows), :] = (scores[pl.ds(start, rows), :] * scale).astype(jnp.bfloat16)
        return carry

    lax.fori_loop(0, ROT, post_step, 0)
    turned_field[...] = lax.dot_general(
        total * scale,
        sw_ref[...],
        (((1,), (1,)), ((), ())),
        precision=lax.Precision.HIGHEST,
        preferred_element_type=jnp.float32,
    ).T

    acc[...] = jnp.zeros_like(acc)
    wide = 2 * SPAN

    def back_step(step, carry):
        base = pl.multiple_of(step * wide, wide)
        oriented = jnp.dot(
            post[...], feats[:, pl.ds(base, wide)], preferred_element_type=jnp.float32
        )
        for turn in range(ROT):
            where = pl.ds(pl.multiple_of(base + (ROT - turn) * SPAN, SPAN), wide)
            acc[:, where] += oriented[turn * rows : (turn + 1) * rows]
        return carry

    lax.fori_loop(0, WIDTH // wide, back_step, 0)
    for q in range(ROT):
        low = acc[:, q * SPAN : (q + 1) * SPAN]
        turned[q * SPAN : (q + 1) * SPAN, :] = (
            low + acc[:, WIDTH + q * SPAN : WIDTH + (q + 1) * SPAN]
        ).T

    def block_for(device):
        parts, weights = [], []
        for index in range(pieces):
            first = device * share + index * piece
            part = lax.div(first, ANG)
            start = lax.rem(first, ANG) * PARTS + part
            parts.append(turned[pl.ds(start, piece, stride=PARTS), :])
            value = turned_field[pl.ds(lax.rem(part, SHELLS), 1), :]
            high = value.astype(jnp.bfloat16).astype(jnp.float32)
            weights += [high, value - high]
        extra = pay.shape[2] - share - len(weights)
        weights.append(jnp.zeros((extra, rows), jnp.float32))
        return jnp.concatenate(parts + weights, axis=0).T.astype(jnp.bfloat16)

    pairs = []
    for offset in [*range(1, half), 0]:
        slot = ahead(offset)
        pay[offset] = block_for(2 * slot + 1 - core)
        copy = remote(
            pay.at[offset], mid.at[offset], pair_send.at[offset], pair_recv.at[offset], partner
        )
        copy.start()
        pairs.append(copy)
    for offset in range(half):
        pay[half + offset] = block_for(2 * ahead(offset) + core)

    lasts = []
    for index, offset in enumerate([*range(1, half), 0]):
        pairs[index].wait_recv()
        value = pay[half + offset].astype(jnp.float32) + mid[offset].astype(jnp.float32)
        if offset:
            lead = value[:, :share]
            tail = value[:, share:]
            mixed[offset, :, :share] = lead.astype(jnp.bfloat16)
            mixed[offset, :, share:] = tail.astype(jnp.bfloat16)
            copy = remote(
                mixed.at[offset],
                final.at[offset],
                last_send.at[offset],
                last_recv.at[offset],
                2 * ahead(offset) + core,
            )
            copy.start()
            lasts.append(copy)
        else:
            result = value
    for index, copy in enumerate(lasts):
        copy.wait_recv()
        result = result + final[index + 1].astype(jnp.float32)
    for index in range(pieces):
        place_w = share + 2 * index
        weights = result[:, place_w : place_w + 1] + result[:, place_w + 1 : place_w + 2]
        out_ref[:, index * piece : (index + 1) * piece] = result[
            :, index * piece : (index + 1) * piece
        ] / (weights + 1.0)
    for copy in pairs + lasts:
        copy.wait_send()


def on_device(images, class_refs, sigma2, ctf_group, defocus_bin):
    count_dev = lax.axis_size("img")
    half = count_dev // 2
    count_img = images.shape[0]
    share = class_refs.shape[1]
    cols = -(-SIDE * SLOTS * count_img // LANES) * LANES
    repeats = SPAN // SHELLS
    filter_weight, shell_weight = image_weights(ctf_group, defocus_bin, sigma2)
    packed = share + 8
    return pl.pallas_call(
        lambda *refs: em_kernel(count_dev, *refs),
        out_shape=jax.ShapeDtypeStruct(class_refs.shape, jnp.float32),
        in_specs=[pl.BlockSpec(memory_space=pltpu.VMEM)] * 5,
        out_specs=pl.BlockSpec(memory_space=pltpu.VMEM),
        scratch_shapes=[
            pltpu.VMEM((cols, WIDTH), jnp.bfloat16),
            pltpu.VMEM((CLASSES, 2 * WIDTH), jnp.bfloat16),
            pltpu.VMEM((ROT * CLASSES, cols), jnp.float32),
            pltpu.VMEM((ROT * CLASSES, cols), jnp.bfloat16),
            pltpu.VMEM((CLASSES, 2 * WIDTH), jnp.float32),
            pltpu.VMEM((WIDTH, count_img), jnp.float32),
            pltpu.VMEM((WIDTH, CLASSES), jnp.float32),
            pltpu.VMEM((SPAN, CLASSES), jnp.float32),
            pltpu.VMEM((4, count_img, WIDTH), jnp.float32),
            pltpu.VMEM((count_dev, CLASSES, share), jnp.bfloat16),
            pltpu.VMEM((count_dev, CLASSES, packed), jnp.bfloat16),
            pltpu.VMEM((half, CLASSES, packed), jnp.bfloat16),
            pltpu.VMEM((half, CLASSES, packed), jnp.bfloat16),
            pltpu.VMEM((half, CLASSES, packed), jnp.bfloat16),
        ]
        + [pltpu.SemaphoreType.DMA((half,))] * 8,
        compiler_params=pltpu.CompilerParams(
            vmem_limit_bytes=60 * 2**20, collective_id=0, has_side_effects=True
        ),
        name="em_step",
    )(
        images,
        class_refs,
        jnp.tile(filter_weight, (1, repeats)),
        jnp.asarray(phase_parts()),
        jnp.tile(shell_weight.T, (repeats, cols // count_img)),
    )


def solution(mesh):
    in_specs = (
        P(("groups", "img"), None),
        P("groups", "img"),
        P("groups", None),
        P(("groups", "img")),
        P(("groups", "img")),
    )
    out_specs = P("groups", "img")
    return jax.shard_map(
        on_device, mesh=mesh, in_specs=in_specs, out_specs=out_specs, check_vma=False
    )
```

```python
import math

import jax
import jax.numpy as jnp
import numpy as np
from jax import lax
from jax.experimental import pallas as pl
from jax.experimental.pallas import tpu as pltpu
from jax.sharding import PartitionSpec as P

CLASSES = 48
ROT = 36
SHELLS = 16
ANG = 144
REACH = 3
SHIFTS = 49
BINS = 32
NGROUP = 16


LANES = 128
PARTS = 2 * SHELLS
SPAN = ANG // ROT * PARTS
WIDTH = ROT * SPAN
SIDE = 2 * REACH + 1
SLOTS = SIDE + 1
BIG = 1e30


def phase_parts():
    offsets = np.arange(SIDE) - REACH
    angles = 2.0 * np.pi * np.arange(ANG) / ANG
    radius = (np.arange(SHELLS) + 1.0) / (2.0 * SHELLS)
    tables = []
    for direction in (np.cos(angles), np.sin(angles)):
        phase = 2.0 * np.pi * offsets[:, None, None] * direction[None, :, None] * radius
        cosine, sine = np.cos(phase), np.sin(phase)
        tables.append(np.stack([cosine, cosine], axis=2).reshape(SIDE, WIDTH))
        tables.append(np.stack([-sine, sine], axis=2).reshape(SIDE, WIDTH))
    return np.stack(tables).astype(np.float32)


def ctf_lanes():
    radius = (np.arange(SHELLS) + 1.0) / (2.0 * SHELLS)
    defocus = 1.0 + np.arange(BINS) / BINS
    table = -np.sin(80.0 * defocus[:, None] * radius**2 + 0.1)
    return np.tile(table, (1, SPAN // SHELLS)).astype(np.float32)


def fold_lanes(row, count_img, combine):
    cols = row.shape[1]
    total = row[:, :LANES]
    for start in range(LANES, cols, LANES):
        total = combine(total, row[:, start : start + LANES])
    reach = count_img
    while reach < LANES:
        total = combine(total, pltpu.roll(total, reach, 1))
        reach *= 2
    return jnp.concatenate([total] * (cols // LANES), axis=1)


def em_kernel(
    count_dev,
    img_ref,
    refs_ref,
    sigma_ref,
    group_ref,
    bin_ref,
    ctf_ref,
    phase_ref,
    out_ref,
    feats,
    twice,
    scores,
    post,
    acc,
    turned_img,
    turned,
    turned_field,
    sw_ref,
    partial,
    got,
    pay,
    mid,
    mixed,
    final,
    near_send,
    near_recv,
    far_send,
    far_recv,
    pair_send,
    pair_recv,
    last_send,
    last_recv,
):
    rows = CLASSES
    count_img = img_ref.shape[0]
    share = refs_ref.shape[1]
    cols = feats.shape[0]
    half = count_dev // 2
    piece = min(share, ANG)
    pieces = share // piece
    me = lax.axis_index("img")
    core = lax.rem(me, 2)
    place = lax.div(me, 2)
    partner = me + 1 - 2 * core

    def ahead(offset):
        return lax.rem(place + offset, half)

    def behind(offset):
        return lax.rem(place + half - offset, half)

    barrier = pltpu.get_barrier_semaphore()
    for offset in range(1, half):
        pl.semaphore_signal(
            barrier,
            inc=1,
            device_id={"img": 2 * ahead(offset) + core},
            device_id_type=pl.DeviceIdType.MESH,
        )
    pl.semaphore_signal(
        barrier, inc=1, device_id={"img": partner}, device_id_type=pl.DeviceIdType.MESH
    )
    pl.semaphore_wait(barrier, half)

    def remote(source, target, send, recv, device):
        return pltpu.make_async_remote_copy(
            src_ref=source,
            dst_ref=target,
            send_sem=send,
            recv_sem=recv,
            device_id={"img": device},
            device_id_type=pl.DeviceIdType.MESH,
        )

    far = [
        remote(
            refs_ref,
            got.at[me],
            far_send.at[offset],
            far_recv.at[offset],
            2 * ahead(offset) + core,
        )
        for offset in range(1, half)
    ]
    near = [remote(refs_ref, got.at[me], near_send.at[0], near_recv.at[0], partner)]
    for copy in far + near:
        copy.start()

    for part in range(PARTS):
        block = img_ref[:, part * ANG : (part + 1) * ANG].astype(jnp.float32)
        turned_img[pl.ds(part, ANG, stride=PARTS), :] = block.T
    repeats = SPAN // SHELLS
    noise = jnp.concatenate([sigma_ref[...]] * repeats, axis=1)

    def pick(ids, table):
        hot = ids == lax.broadcasted_iota(jnp.int32, (table.shape[0], count_img), 0)
        return lax.dot_general(
            hot.astype(jnp.float32),
            table,
            (((0,), (0,)), ((), ())),
            precision=lax.Precision.HIGHEST,
            preferred_element_type=jnp.float32,
        )

    ctf = pick(bin_ref[...], ctf_ref[...])
    noise = pick(group_ref[...], noise)
    weight = ctf / noise
    image_col = lax.rem(lax.broadcasted_iota(jnp.int32, (count_img, cols), 1), count_img)
    image_hot = image_col == lax.broadcasted_iota(jnp.int32, (count_img, cols), 0)
    sw_ref[...] = lax.dot_general(
        ctf * ctf / noise,
        image_hot.astype(jnp.float32),
        (((0,), (0,)), ((), ())),
        precision=lax.Precision.HIGHEST,
        preferred_element_type=jnp.float32,
    )
    lane = lax.broadcasted_iota(jnp.int32, (count_img, WIDTH), 1)
    real_lane = lax.rem(lane, PARTS) < SHELLS

    def swap(value):
        return jnp.where(
            real_lane, pltpu.roll(value, WIDTH - SHELLS, 1), pltpu.roll(value, SHELLS, 1)
        )

    filtered = jnp.concatenate(
        [turned_img[q * SPAN : (q + 1) * SPAN, :].T * weight for q in range(ROT)], axis=1
    )
    partial[0] = filtered
    partial[1] = swap(filtered)
    group = SLOTS * count_img

    def feature_step(step, carry):
        moved = (
            partial[0] * phase_ref[0, pl.ds(step, 1), :]
            + partial[1] * phase_ref[1, pl.ds(step, 1), :]
        )
        partial[2] = moved
        partial[3] = swap(moved)
        start = pl.multiple_of(step * group, group)
        for slot in range(0, SLOTS, 2):
            pair = []
            for shift in (slot, slot + 1):
                if shift < SIDE:
                    pair.append(
                        partial[2] * phase_ref[2, shift : shift + 1, :]
                        + partial[3] * phase_ref[3, shift : shift + 1, :]
                    )
                else:
                    pair.append(jnp.zeros((count_img, WIDTH), jnp.float32))
            feats[pl.ds(start + slot * count_img, 2 * count_img), :] = jnp.concatenate(
                pair, axis=0
            ).astype(jnp.bfloat16)
        return carry

    lax.fori_loop(0, SIDE, feature_step, 0)
    feats[SIDE * group :, :] = jnp.zeros((cols - SIDE * group, WIDTH), jnp.bfloat16)

    def place_refs(block, source):
        block = block.astype(jnp.float32)
        for index in range(pieces):
            first = source * share + index * piece
            start = lax.rem(first, ANG) * PARTS + lax.div(first, ANG)
            turned[pl.ds(start, piece, stride=PARTS), :] = block[
                :, index * piece : (index + 1) * piece
            ].T

    place_refs(refs_ref[...], me)
    for offset in range(1, half):
        source = 2 * behind(offset) + core
        far[offset - 1].wait_recv()
        copy = remote(
            got.at[source], got.at[source], near_send.at[offset], near_recv.at[offset], partner
        )
        copy.start()
        near.append(copy)
        place_refs(got[source], source)
    for offset in range(half):
        source = 2 * behind(offset) + 1 - core
        near[offset].wait_recv()
        place_refs(got[source], source)
    for copy in far + near:
        copy.wait_send()

    power = jnp.zeros((rows, SPAN), jnp.float32)
    for q in range(ROT):
        block = turned[q * SPAN : (q + 1) * SPAN, :].T
        power = power + block * block
        block = block.astype(jnp.bfloat16)
        twice[:, q * SPAN : (q + 1) * SPAN] = block
        twice[:, WIDTH + q * SPAN : WIDTH + (q + 1) * SPAN] = block
    quad = 0.5 * lax.dot_general(
        power,
        sw_ref[...],
        (((1,), (0,)), ((), ())),
        precision=lax.Precision.HIGHEST,
        preferred_element_type=jnp.float32,
    )
    col = lax.broadcasted_iota(jnp.int32, (rows, cols), 1)
    used = (lax.rem(col, group) < SIDE * count_img) & (col < SIDE * group)
    quad = jnp.where(used, quad, BIG)

    depth = 4 * SPAN
    for turn in range(ROT):
        scores[turn * rows : (turn + 1) * rows, :] = -quad

    def cross_step(step, carry):
        base = pl.multiple_of(step * depth, depth)
        left = jnp.concatenate(
            [
                twice[:, pl.ds(pl.multiple_of(base + (ROT - turn) * SPAN, SPAN), depth)]
                for turn in range(ROT)
            ],
            axis=0,
        )
        scores[...] += lax.dot_general(
            left,
            feats[:, pl.ds(base, depth)],
            (((1,), (1,)), ((), ())),
            preferred_element_type=jnp.float32,
        )
        return carry

    lax.fori_loop(0, WIDTH // depth, cross_step, 0)

    def max_step(turn, best):
        start = pl.multiple_of(turn * rows, rows)
        return jnp.maximum(best, scores[pl.ds(start, rows), :])

    best = lax.fori_loop(0, ROT, max_step, jnp.full((rows, cols), -BIG, jnp.float32))
    top = fold_lanes(jnp.max(best, axis=0, keepdims=True), count_img, jnp.maximum)

    def exp_step(turn, total):
        start = pl.multiple_of(turn * rows, rows)
        value = jnp.exp(scores[pl.ds(start, rows), :] - top)
        scores[pl.ds(start, rows), :] = value
        return total + value

    total = lax.fori_loop(0, ROT, exp_step, jnp.zeros((rows, cols), jnp.float32))
    norm = fold_lanes(jnp.sum(total, axis=0, keepdims=True), count_img, jnp.add)
    scale = 1.0 / norm

    def post_step(turn, carry):
        start = pl.multiple_of(turn * rows, rows)
        post[pl.ds(start, rows), :] = (scores[pl.ds(start, rows), :] * scale).astype(jnp.bfloat16)
        return carry

    lax.fori_loop(0, ROT, post_step, 0)
    turned_field[...] = lax.dot_general(
        total * scale,
        sw_ref[...],
        (((1,), (1,)), ((), ())),
        precision=lax.Precision.HIGHEST,
        preferred_element_type=jnp.float32,
    ).T

    acc[...] = jnp.zeros_like(acc)
    wide = 2 * SPAN

    def back_step(step, carry):
        base = pl.multiple_of(step * wide, wide)
        oriented = jnp.dot(
            post[...], feats[:, pl.ds(base, wide)], preferred_element_type=jnp.float32
        )
        for turn in range(ROT):
            where = pl.ds(pl.multiple_of(base + (ROT - turn) * SPAN, SPAN), wide)
            acc[:, where] += oriented[turn * rows : (turn + 1) * rows]
        return carry

    lax.fori_loop(0, WIDTH // wide, back_step, 0)
    for q in range(ROT):
        low = acc[:, q * SPAN : (q + 1) * SPAN]
        turned[q * SPAN : (q + 1) * SPAN, :] = (
            low + acc[:, WIDTH + q * SPAN : WIDTH + (q + 1) * SPAN]
        ).T

    def block_for(device):
        parts, weights = [], []
        for index in range(pieces):
            first = device * share + index * piece
            part = lax.div(first, ANG)
            start = lax.rem(first, ANG) * PARTS + part
            parts.append(turned[pl.ds(start, piece, stride=PARTS), :])
            value = turned_field[pl.ds(lax.rem(part, SHELLS), 1), :]
            high = value.astype(jnp.bfloat16).astype(jnp.float32)
            weights += [high, value - high]
        extra = pay.shape[2] - share - len(weights)
        weights.append(jnp.zeros((extra, rows), jnp.float32))
        return jnp.concatenate(parts + weights, axis=0).T

    pairs = []
    for offset in [*range(1, half), 0]:
        slot = ahead(offset)
        pay[offset] = block_for(2 * slot + 1 - core).astype(jnp.bfloat16)
        copy = remote(
            pay.at[offset], mid.at[offset], pair_send.at[offset], pair_recv.at[offset], partner
        )
        copy.start()
        pairs.append(copy)

    lasts = []
    for index, offset in enumerate([*range(1, half), 0]):
        own = block_for(2 * ahead(offset) + core)
        pairs[index].wait_recv()
        value = own + mid[offset].astype(jnp.float32)
        if offset:
            mixed[offset] = value.astype(jnp.bfloat16)
            copy = remote(
                mixed.at[offset],
                final.at[offset],
                last_send.at[offset],
                last_recv.at[offset],
                2 * ahead(offset) + core,
            )
            copy.start()
            lasts.append(copy)
        else:
            result = value
    for index, copy in enumerate(lasts):
        copy.wait_recv()
        result = result + final[index + 1].astype(jnp.float32)
    for index in range(pieces):
        place_w = share + 2 * index
        weights = result[:, place_w : place_w + 1] + result[:, place_w + 1 : place_w + 2]
        out_ref[:, index * piece : (index + 1) * piece] = result[
            :, index * piece : (index + 1) * piece
        ] / (weights + 1.0)
    for copy in pairs + lasts:
        copy.wait_send()


def on_device(images, class_refs, sigma2, ctf_group, defocus_bin):
    count_dev = lax.axis_size("img")
    half = count_dev // 2
    count_img = images.shape[0]
    share = class_refs.shape[1]
    cols = -(-SIDE * SLOTS * count_img // LANES) * LANES
    packed = share + 8
    return pl.pallas_call(
        lambda *refs: em_kernel(count_dev, *refs),
        out_shape=jax.ShapeDtypeStruct(class_refs.shape, jnp.float32),
        in_specs=[pl.BlockSpec(memory_space=pltpu.VMEM)] * 7,
        out_specs=pl.BlockSpec(memory_space=pltpu.VMEM),
        scratch_shapes=[
            pltpu.VMEM((cols, WIDTH), jnp.bfloat16),
            pltpu.VMEM((CLASSES, 2 * WIDTH), jnp.bfloat16),
            pltpu.VMEM((ROT * CLASSES, cols), jnp.float32),
            pltpu.VMEM((ROT * CLASSES, cols), jnp.bfloat16),
            pltpu.VMEM((CLASSES, 2 * WIDTH), jnp.float32),
            pltpu.VMEM((WIDTH, count_img), jnp.float32),
            pltpu.VMEM((WIDTH, CLASSES), jnp.float32),
            pltpu.VMEM((SPAN, CLASSES), jnp.float32),
            pltpu.VMEM((SPAN, cols), jnp.float32),
            pltpu.VMEM((4, count_img, WIDTH), jnp.float32),
            pltpu.VMEM((count_dev, CLASSES, share), jnp.bfloat16),
            pltpu.VMEM((half, CLASSES, packed), jnp.bfloat16),
            pltpu.VMEM((half, CLASSES, packed), jnp.bfloat16),
            pltpu.VMEM((half, CLASSES, packed), jnp.bfloat16),
            pltpu.VMEM((half, CLASSES, packed), jnp.bfloat16),
        ]
        + [pltpu.SemaphoreType.DMA((half,))] * 8,
        compiler_params=pltpu.CompilerParams(
            vmem_limit_bytes=60 * 2**20, collective_id=0, has_side_effects=True
        ),
        name="em_step",
    )(
        images,
        class_refs,
        sigma2,
        ctf_group.reshape(1, count_img),
        defocus_bin.reshape(1, count_img),
        jnp.asarray(ctf_lanes()),
        jnp.asarray(phase_parts()),
    )


def solution(mesh):
    in_specs = (
        P(("groups", "img"), None),
        P("groups", "img"),
        P("groups", None),
        P(("groups", "img")),
        P(("groups", "img")),
    )
    out_specs = P("groups", "img")
    return jax.shard_map(
        on_device, mesh=mesh, in_specs=in_specs, out_specs=out_specs, check_vma=False
    )
```

```python
import math

import jax
import jax.numpy as jnp
import numpy as np
from jax import lax
from jax.experimental import pallas as pl
from jax.experimental.pallas import tpu as pltpu
from jax.sharding import PartitionSpec as P

CLASSES = 48
ROT = 36
SHELLS = 16
ANG = 144
REACH = 3
SHIFTS = 49
BINS = 32
NGROUP = 16


LANES = 128
PARTS = 2 * SHELLS
SPAN = ANG // ROT * PARTS
WIDTH = ROT * SPAN
SIDE = 2 * REACH + 1
SLOTS = SIDE + 1
BIG = 1e30


def phase_parts():
    offsets = np.arange(SIDE) - REACH
    angles = 2.0 * np.pi * np.arange(ANG) / ANG
    radius = (np.arange(SHELLS) + 1.0) / (2.0 * SHELLS)
    tables = []
    for direction in (np.cos(angles), np.sin(angles)):
        phase = 2.0 * np.pi * offsets[:, None, None] * direction[None, :, None] * radius
        cosine, sine = np.cos(phase), np.sin(phase)
        tables.append(np.stack([cosine, cosine], axis=2).reshape(SIDE, WIDTH))
        tables.append(np.stack([-sine, sine], axis=2).reshape(SIDE, WIDTH))
    return np.stack(tables).astype(np.float32)


def ctf_lanes():
    radius = (np.arange(SHELLS) + 1.0) / (2.0 * SHELLS)
    defocus = 1.0 + np.arange(BINS) / BINS
    table = -np.sin(80.0 * defocus[:, None] * radius**2 + 0.1)
    return np.tile(table, (1, SPAN // SHELLS)).astype(np.float32)


def fold_lanes(row, count_img, combine):
    cols = row.shape[1]
    total = row[:, :LANES]
    for start in range(LANES, cols, LANES):
        total = combine(total, row[:, start : start + LANES])
    reach = count_img
    while reach < LANES:
        total = combine(total, pltpu.roll(total, reach, 1))
        reach *= 2
    return jnp.concatenate([total] * (cols // LANES), axis=1)


def packing(width):
    full, tail = width // LANES, width % LANES
    groups = 3 if tail and 3 * tail <= LANES and CLASSES % 48 == 0 else 1
    return full, tail, groups


def packed_rows(width):
    full, tail, groups = packing(width)
    return full * CLASSES + (CLASSES // groups if tail else 0)


def pack(block):
    full, tail, groups = packing(block.shape[1])
    columns = [block[:, index * LANES : (index + 1) * LANES] for index in range(full)]
    if tail:
        rest = block[:, full * LANES :]
        size = CLASSES // groups
        pieces = [rest[index * size : (index + 1) * size] for index in range(groups)]
        spare = LANES - groups * tail
        if spare:
            pieces.append(jnp.zeros((size, spare), block.dtype))
        columns.append(jnp.concatenate(pieces, axis=1))
    return jnp.concatenate(columns, axis=0)


def unpack(block, width):
    full, tail, groups = packing(width)
    columns = [block[index * CLASSES : (index + 1) * CLASSES] for index in range(full)]
    if tail:
        rest = block[full * CLASSES :]
        columns.append(
            jnp.concatenate(
                [rest[:, index * tail : (index + 1) * tail] for index in range(groups)], axis=0
            )
        )
    return jnp.concatenate(columns, axis=1)


def em_kernel(
    count_dev,
    img_ref,
    refs_ref,
    sigma_ref,
    group_ref,
    bin_ref,
    ctf_ref,
    phase_ref,
    out_ref,
    feats,
    twice,
    scores,
    post,
    acc,
    turned_img,
    turned,
    turned_field,
    sw_ref,
    partial,
    mine,
    got,
    pay,
    mid,
    mixed,
    final,
    near_send,
    near_recv,
    far_send,
    far_recv,
    pair_send,
    pair_recv,
    last_send,
    last_recv,
):
    rows = CLASSES
    count_img = img_ref.shape[0]
    share = refs_ref.shape[1]
    cols = feats.shape[0]
    half = count_dev // 2
    packed = share + 8
    piece = min(share, ANG)
    pieces = share // piece
    me = lax.axis_index("img")
    core = lax.rem(me, 2)
    place = lax.div(me, 2)
    partner = me + 1 - 2 * core

    def ahead(offset):
        return lax.rem(place + offset, half)

    def behind(offset):
        return lax.rem(place + half - offset, half)

    barrier = pltpu.get_barrier_semaphore()
    for offset in range(1, half):
        pl.semaphore_signal(
            barrier,
            inc=1,
            device_id={"img": 2 * ahead(offset) + core},
            device_id_type=pl.DeviceIdType.MESH,
        )
    pl.semaphore_signal(
        barrier, inc=1, device_id={"img": partner}, device_id_type=pl.DeviceIdType.MESH
    )
    pl.semaphore_wait(barrier, half)

    def remote(source, target, send, recv, device):
        return pltpu.make_async_remote_copy(
            src_ref=source,
            dst_ref=target,
            send_sem=send,
            recv_sem=recv,
            device_id={"img": device},
            device_id_type=pl.DeviceIdType.MESH,
        )

    mine[...] = pack(refs_ref[...].astype(jnp.float32)).astype(jnp.bfloat16)

    far = [
        remote(
            mine,
            got.at[me],
            far_send.at[offset],
            far_recv.at[offset],
            2 * ahead(offset) + core,
        )
        for offset in range(1, half)
    ]
    near = [remote(mine, got.at[me], near_send.at[0], near_recv.at[0], partner)]
    for copy in far + near:
        copy.start()

    for part in range(PARTS):
        block = img_ref[:, part * ANG : (part + 1) * ANG].astype(jnp.float32)
        turned_img[pl.ds(part, ANG, stride=PARTS), :] = block.T
    repeats = SPAN // SHELLS
    noise = jnp.concatenate([sigma_ref[...]] * repeats, axis=1)

    def pick(ids, table):
        hot = ids == lax.broadcasted_iota(jnp.int32, (table.shape[0], count_img), 0)
        return lax.dot_general(
            hot.astype(jnp.float32),
            table,
            (((0,), (0,)), ((), ())),
            precision=lax.Precision.HIGHEST,
            preferred_element_type=jnp.float32,
        )

    ctf = pick(bin_ref[...], ctf_ref[...])
    noise = pick(group_ref[...], noise)
    weight = ctf / noise
    image_col = lax.rem(lax.broadcasted_iota(jnp.int32, (count_img, cols), 1), count_img)
    image_hot = image_col == lax.broadcasted_iota(jnp.int32, (count_img, cols), 0)
    sw_ref[...] = lax.dot_general(
        ctf * ctf / noise,
        image_hot.astype(jnp.float32),
        (((0,), (0,)), ((), ())),
        precision=lax.Precision.HIGHEST,
        preferred_element_type=jnp.float32,
    )
    lane = lax.broadcasted_iota(jnp.int32, (count_img, WIDTH), 1)
    real_lane = lax.rem(lane, PARTS) < SHELLS

    def swap(value):
        return jnp.where(
            real_lane, pltpu.roll(value, WIDTH - SHELLS, 1), pltpu.roll(value, SHELLS, 1)
        )

    filtered = jnp.concatenate(
        [turned_img[q * SPAN : (q + 1) * SPAN, :].T * weight for q in range(ROT)], axis=1
    )
    partial[0] = filtered
    partial[1] = swap(filtered)
    group = SLOTS * count_img

    def feature_step(step, carry):
        moved = (
            partial[0] * phase_ref[0, pl.ds(step, 1), :]
            + partial[1] * phase_ref[1, pl.ds(step, 1), :]
        )
        partial[2] = moved
        partial[3] = swap(moved)
        start = pl.multiple_of(step * group, group)
        for slot in range(0, SLOTS, 2):
            pair = []
            for shift in (slot, slot + 1):
                if shift < SIDE:
                    pair.append(
                        partial[2] * phase_ref[2, shift : shift + 1, :]
                        + partial[3] * phase_ref[3, shift : shift + 1, :]
                    )
                else:
                    pair.append(jnp.zeros((count_img, WIDTH), jnp.float32))
            feats[pl.ds(start + slot * count_img, 2 * count_img), :] = jnp.concatenate(
                pair, axis=0
            ).astype(jnp.bfloat16)
        return carry

    lax.fori_loop(0, SIDE, feature_step, 0)
    feats[SIDE * group :, :] = jnp.zeros((cols - SIDE * group, WIDTH), jnp.bfloat16)

    def place_refs(block, source):
        for index in range(pieces):
            first = source * share + index * piece
            start = lax.rem(first, ANG) * PARTS + lax.div(first, ANG)
            turned[pl.ds(start, piece, stride=PARTS), :] = block[
                :, index * piece : (index + 1) * piece
            ].T

    place_refs(refs_ref[...].astype(jnp.float32), me)
    for offset in range(1, half):
        source = 2 * behind(offset) + core
        far[offset - 1].wait_recv()
        copy = remote(
            got.at[source], got.at[source], near_send.at[offset], near_recv.at[offset], partner
        )
        copy.start()
        near.append(copy)
        place_refs(unpack(got[source].astype(jnp.float32), share), source)
    for offset in range(half):
        source = 2 * behind(offset) + 1 - core
        near[offset].wait_recv()
        place_refs(unpack(got[source].astype(jnp.float32), share), source)
    for copy in far + near:
        copy.wait_send()

    power = jnp.zeros((rows, SPAN), jnp.float32)
    for q in range(ROT):
        block = turned[q * SPAN : (q + 1) * SPAN, :].T
        power = power + block * block
        block = block.astype(jnp.bfloat16)
        twice[:, q * SPAN : (q + 1) * SPAN] = block
        twice[:, WIDTH + q * SPAN : WIDTH + (q + 1) * SPAN] = block
    quad = 0.5 * lax.dot_general(
        power,
        sw_ref[...],
        (((1,), (0,)), ((), ())),
        precision=lax.Precision.HIGHEST,
        preferred_element_type=jnp.float32,
    )
    col = lax.broadcasted_iota(jnp.int32, (rows, cols), 1)
    used = (lax.rem(col, group) < SIDE * count_img) & (col < SIDE * group)
    quad = jnp.where(used, quad, BIG)

    depth = 4 * SPAN
    for turn in range(ROT):
        scores[turn * rows : (turn + 1) * rows, :] = -quad

    def cross_step(step, carry):
        base = pl.multiple_of(step * depth, depth)
        left = jnp.concatenate(
            [
                twice[:, pl.ds(pl.multiple_of(base + (ROT - turn) * SPAN, SPAN), depth)]
                for turn in range(ROT)
            ],
            axis=0,
        )
        scores[...] += lax.dot_general(
            left,
            feats[:, pl.ds(base, depth)],
            (((1,), (1,)), ((), ())),
            preferred_element_type=jnp.float32,
        )
        return carry

    lax.fori_loop(0, WIDTH // depth, cross_step, 0)

    def max_step(turn, best):
        start = pl.multiple_of(turn * rows, rows)
        return jnp.maximum(best, scores[pl.ds(start, rows), :])

    best = lax.fori_loop(0, ROT, max_step, jnp.full((rows, cols), -BIG, jnp.float32))
    top = fold_lanes(jnp.max(best, axis=0, keepdims=True), count_img, jnp.maximum)

    def exp_step(turn, total):
        start = pl.multiple_of(turn * rows, rows)
        value = jnp.exp(scores[pl.ds(start, rows), :] - top)
        scores[pl.ds(start, rows), :] = value
        return total + value

    total = lax.fori_loop(0, ROT, exp_step, jnp.zeros((rows, cols), jnp.float32))
    norm = fold_lanes(jnp.sum(total, axis=0, keepdims=True), count_img, jnp.add)
    scale = 1.0 / norm

    def post_step(turn, carry):
        start = pl.multiple_of(turn * rows, rows)
        post[pl.ds(start, rows), :] = (scores[pl.ds(start, rows), :] * scale).astype(jnp.bfloat16)
        return carry

    lax.fori_loop(0, ROT, post_step, 0)
    turned_field[...] = lax.dot_general(
        total * scale,
        sw_ref[...],
        (((1,), (1,)), ((), ())),
        precision=lax.Precision.HIGHEST,
        preferred_element_type=jnp.float32,
    ).T

    acc[...] = jnp.zeros_like(acc)
    wide = 2 * SPAN

    def back_step(step, carry):
        base = pl.multiple_of(step * wide, wide)
        oriented = jnp.dot(
            post[...], feats[:, pl.ds(base, wide)], preferred_element_type=jnp.float32
        )
        for turn in range(ROT):
            where = pl.ds(pl.multiple_of(base + (ROT - turn) * SPAN, SPAN), wide)
            acc[:, where] += oriented[turn * rows : (turn + 1) * rows]
        return carry

    lax.fori_loop(0, WIDTH // wide, back_step, 0)
    for q in range(ROT):
        low = acc[:, q * SPAN : (q + 1) * SPAN]
        turned[q * SPAN : (q + 1) * SPAN, :] = (
            low + acc[:, WIDTH + q * SPAN : WIDTH + (q + 1) * SPAN]
        ).T

    def block_for(device):
        parts, weights = [], []
        for index in range(pieces):
            first = device * share + index * piece
            part = lax.div(first, ANG)
            start = lax.rem(first, ANG) * PARTS + part
            parts.append(turned[pl.ds(start, piece, stride=PARTS), :])
            value = turned_field[pl.ds(lax.rem(part, SHELLS), 1), :]
            high = value.astype(jnp.bfloat16).astype(jnp.float32)
            weights += [high, value - high]
        extra = packed - share - len(weights)
        weights.append(jnp.zeros((extra, rows), jnp.float32))
        return jnp.concatenate(parts + weights, axis=0).T

    pairs = []
    for offset in [*range(1, half), 0]:
        slot = ahead(offset)
        pay[offset] = pack(block_for(2 * slot + 1 - core)).astype(jnp.bfloat16)
        copy = remote(
            pay.at[offset], mid.at[offset], pair_send.at[offset], pair_recv.at[offset], partner
        )
        copy.start()
        pairs.append(copy)

    lasts = []
    for index, offset in enumerate([*range(1, half), 0]):
        own = pack(block_for(2 * ahead(offset) + core))
        pairs[index].wait_recv()
        value = own + mid[offset].astype(jnp.float32)
        if offset:
            mixed[offset] = value.astype(jnp.bfloat16)
            copy = remote(
                mixed.at[offset],
                final.at[offset],
                last_send.at[offset],
                last_recv.at[offset],
                2 * ahead(offset) + core,
            )
            copy.start()
            lasts.append(copy)
        else:
            result = value
    for index, copy in enumerate(lasts):
        copy.wait_recv()
        result = result + final[index + 1].astype(jnp.float32)
    result = unpack(result, packed)
    for index in range(pieces):
        place_w = share + 2 * index
        weights = result[:, place_w : place_w + 1] + result[:, place_w + 1 : place_w + 2]
        out_ref[:, index * piece : (index + 1) * piece] = result[
            :, index * piece : (index + 1) * piece
        ] / (weights + 1.0)
    for copy in pairs + lasts:
        copy.wait_send()


def on_device(images, class_refs, sigma2, ctf_group, defocus_bin):
    count_dev = lax.axis_size("img")
    half = count_dev // 2
    count_img = images.shape[0]
    share = class_refs.shape[1]
    cols = -(-SIDE * SLOTS * count_img // LANES) * LANES
    packed = share + 8
    return pl.pallas_call(
        lambda *refs: em_kernel(count_dev, *refs),
        out_shape=jax.ShapeDtypeStruct(class_refs.shape, jnp.float32),
        in_specs=[pl.BlockSpec(memory_space=pltpu.VMEM)] * 7,
        out_specs=pl.BlockSpec(memory_space=pltpu.VMEM),
        scratch_shapes=[
            pltpu.VMEM((cols, WIDTH), jnp.bfloat16),
            pltpu.VMEM((CLASSES, 2 * WIDTH), jnp.bfloat16),
            pltpu.VMEM((ROT * CLASSES, cols), jnp.float32),
            pltpu.VMEM((ROT * CLASSES, cols), jnp.bfloat16),
            pltpu.VMEM((CLASSES, 2 * WIDTH), jnp.float32),
            pltpu.VMEM((WIDTH, count_img), jnp.float32),
            pltpu.VMEM((WIDTH, CLASSES), jnp.float32),
            pltpu.VMEM((SPAN, CLASSES), jnp.float32),
            pltpu.VMEM((SPAN, cols), jnp.float32),
            pltpu.VMEM((4, count_img, WIDTH), jnp.float32),
            pltpu.VMEM((packed_rows(share), LANES), jnp.bfloat16),
            pltpu.VMEM((count_dev, packed_rows(share), LANES), jnp.bfloat16),
            pltpu.VMEM((half, packed_rows(packed), LANES), jnp.bfloat16),
            pltpu.VMEM((half, packed_rows(packed), LANES), jnp.bfloat16),
            pltpu.VMEM((half, packed_rows(packed), LANES), jnp.bfloat16),
            pltpu.VMEM((half, packed_rows(packed), LANES), jnp.bfloat16),
        ]
        + [pltpu.SemaphoreType.DMA((half,))] * 8,
        compiler_params=pltpu.CompilerParams(
            vmem_limit_bytes=60 * 2**20, collective_id=0, has_side_effects=True
        ),
        name="em_step",
    )(
        images,
        class_refs,
        sigma2,
        ctf_group.reshape(1, count_img),
        defocus_bin.reshape(1, count_img),
        jnp.asarray(ctf_lanes()),
        jnp.asarray(phase_parts()),
    )


def solution(mesh):
    in_specs = (
        P(("groups", "img"), None),
        P("groups", "img"),
        P("groups", None),
        P(("groups", "img")),
        P(("groups", "img")),
    )
    out_specs = P("groups", "img")
    return jax.shard_map(
        on_device, mesh=mesh, in_specs=in_specs, out_specs=out_specs, check_vma=False
    )
```
